512 devices in a mesh: dp: 32 (over y, z_lo), tensor: 16 (over z_hi, x, core).
Axes of the slice: x: 4, y: 4, z: 16 (z_hi: 2, z_lo: 8; z = z_hi * 8 + z_lo), core: 2. Of those that a mesh axis runs over, the one named last changes fastest.
Arguments:
- output_gradient: bfloat16 [12288, 8192], P(('dp', 'tensor')), may hold values from -6 to 6
- attention_output: bfloat16 [12288, 8192], P('dp', 'tensor'), may hold values from -0.29882812 to 0.29882812
- frozen_projection: bfloat16 [8192, 8192], P('tensor', 'dp'), may hold values from -0.0625 to 0.0625
- domain_down_map: bfloat16 [4, 32, 8192], P(None, None, 'tensor'), may hold values from -0.29882812 to 0.29882812
- domain_up_map: bfloat16 [4, 32, 8192], P(None, None, 'tensor'), may hold values from -0.0625 to 0.0625
- common_down_map: bfloat16 [16, 8192], P(None, 'tensor'), may hold values from -0.29882812 to 0.29882812
- common_up_map: bfloat16 [16, 8192], P(None, 'tensor'), may hold values from -0.0625 to 0.0625
- live_token_count: int32 [32], P('dp'), may hold values from 128 to 384, as said below
- series_domain: int32 [32], replicated, may hold values from 0 to 3, as said below
Outputs:
- grad_input: bfloat16 [12288, 8192], P('dp', 'tensor')
- domain_down_gradient: float32 [4, 32, 8192], P(None, None, 'tensor')
- domain_up_gradient: float32 [4, 32, 8192], P(None, None, 'tensor')
- common_down_gradient: float32 [16, 8192], P(None, 'tensor')
- common_up_gradient: float32 [16, 8192], P(None, 'tensor')
The draws below stay inside these ranges and needn't reach their ends.
Inputs may be any that keep to these rules, and one draw needn't show every extreme that they name: `live_token_count`: a multiple of 128; some series has exactly 384. `series_domain`: every domain is named by at least one series.
All inputs are finite; a program needn't handle non-finite values.
Results may differ from the reference program's by a relative error of at most 0.0035.
Values may be sent and summed in bfloat16 or wider, within the bound.
No kernel may reach another device: no remote copies, remote signals or barrier semaphores. Data moves between devices by JAX's collectives and lax.ppermute only.
A program may use at most 64 MiB of HBM per device.

```python
import jax
import jax.numpy as jnp
from jax import lax

MODEL_WIDTH = 8192
QUERY_HEAD_WIDTH = 8192
ADAPTER_RANK = 32
SRANK = 16
DOMAIN_COUNT = 4
BLOCK = 128
SERIES_TOKENS = 384
ALL_TOK = 12288
N_DP = 32


def draw_live_token_count(key, part):
    blocks_all = SERIES_TOKENS // BLOCK
    rank_ids = jnp.arange(N_DP, dtype=jnp.int32)
    extra_blocks = jax.random.randint(jax.random.fold_in(key, 11), (N_DP,), 0, 2)
    blocks = jnp.minimum(blocks_all, 1 + rank_ids * blocks_all // N_DP + extra_blocks)
    return (blocks * BLOCK).astype(jnp.int32)


def draw_series_domain(key, part):
    shuffled = jax.random.permutation(jax.random.fold_in(key, 21), N_DP)
    first_draw = jax.random.randint(jax.random.fold_in(key, 22), (N_DP,), 0, DOMAIN_COUNT)
    second_draw = jax.random.randint(jax.random.fold_in(key, 23), (N_DP,), 0, DOMAIN_COUNT)
    skewed = jnp.minimum(first_draw, second_draw).astype(jnp.int32)
    return skewed.at[shuffled[:DOMAIN_COUNT]].set(jnp.arange(DOMAIN_COUNT, dtype=jnp.int32)).astype(jnp.int32)


def block_levels(own_key, extent, shards, least, largest):
    loudness, own = 1.0, jax.random.fold_in(own_key, 6)
    for axis_at, shards_of in shards:
        draws = jnp.exp(jax.random.uniform(jax.random.fold_in(own, axis_at), (shards_of,), jnp.float32, least / len(shards), largest / len(shards)))
        loudness = loudness * jnp.repeat(draws, extent[axis_at] // shards_of).reshape([-1 if axis == axis_at else 1 for axis in range(len(extent))])
    return loudness


def gaussian(rng, extent, deviation, limit, split=(), kind=jnp.bfloat16):
    result = jax.random.normal(rng, extent, jnp.float32) * deviation
    if len(split) > 0:
        result = block_levels(rng, extent, split, -0.22, 0.18) * result
    return jnp.clip(result, min=-limit, max=limit).astype(kind)


def setup_inputs(seed: int = 0) -> dict:
    splits = jax.random.split(jax.random.key(seed), 10)
    output_gradient = gaussian(splits[0], (ALL_TOK, MODEL_WIDTH), 1.0, 6.0, ((0, 512),))
    attention_output = gaussian(splits[1], (ALL_TOK, QUERY_HEAD_WIDTH), 0.05, 0.29882812, ((0, 32), (1, 16)))
    frozen_projection = gaussian(splits[2], (QUERY_HEAD_WIDTH, MODEL_WIDTH), MODEL_WIDTH ** -0.5, 0.0625, ((0, 16), (1, 32)))
    domain_down_map = gaussian(splits[3], (DOMAIN_COUNT, ADAPTER_RANK, QUERY_HEAD_WIDTH), 0.05, 0.29882812, ((2, 16),))
    domain_up_map = gaussian(splits[4], (DOMAIN_COUNT, ADAPTER_RANK, MODEL_WIDTH), MODEL_WIDTH ** -0.5, 0.0625, ((2, 16),))
    common_down_map = gaussian(splits[5], (SRANK, QUERY_HEAD_WIDTH), 0.05, 0.29882812, ((1, 16),))
    common_up_map = gaussian(splits[6], (SRANK, MODEL_WIDTH), MODEL_WIDTH ** -0.5, 0.0625, ((1, 16),))
    live_token_count = draw_live_token_count(jax.random.fold_in(splits[9], 71), 0)
    series_domain = draw_series_domain(jax.random.fold_in(splits[9], 71), 0)
    return {"output_gradient": output_gradient, "attention_output": attention_output, "frozen_projection": frozen_projection, "domain_down_map": domain_down_map, "domain_up_map": domain_up_map, "common_down_map": common_down_map, "common_up_map": common_up_map, "live_token_count": live_token_count, "series_domain": series_domain}


adapter_scale = 2.0
shared_scale = 2.0


def reference(output_gradient, attention_output, frozen_projection, domain_down_map, domain_up_map, common_down_map, common_up_map, live_token_count, series_domain):
    grad_seq = output_gradient.reshape(N_DP, SERIES_TOKENS, MODEL_WIDTH)
    act_seq = attention_output.reshape(N_DP, SERIES_TOKENS, QUERY_HEAD_WIDTH)
    positions = lax.iota(jnp.int32, SERIES_TOKENS)
    live_rows = positions[None, :] < live_token_count[:, None]
    masked = jnp.where(live_rows[:, :, None], grad_seq, jnp.zeros_like(grad_seq))

    def per_rank(operands):
        gradient_rows, activation_rows, domain_label = operands
        local_down_map = lax.dynamic_index_in_dim(domain_down_map, domain_label, 0, keepdims=False)
        local_up_map = lax.dynamic_index_in_dim(domain_up_map, domain_label, 0, keepdims=False)
        reduced_activation = jnp.dot(activation_rows, local_down_map.T, preferred_element_type=jnp.float32).astype(jnp.bfloat16)
        low_shared = jnp.dot(activation_rows, common_down_map.T, preferred_element_type=jnp.float32).astype(jnp.bfloat16)
        domain_backward = jnp.dot(gradient_rows, local_up_map.T, preferred_element_type=jnp.float32).astype(jnp.bfloat16)
        back_shared = jnp.dot(gradient_rows, common_up_map.T, preferred_element_type=jnp.float32).astype(jnp.bfloat16)
        input_gradient = jnp.dot(gradient_rows, frozen_projection.T, preferred_element_type=jnp.float32)
        input_gradient = input_gradient + adapter_scale * jnp.dot(domain_backward, local_down_map, preferred_element_type=jnp.float32)
        input_gradient = input_gradient + shared_scale * jnp.dot(back_shared, common_down_map, preferred_element_type=jnp.float32)
        down_gradient = adapter_scale * jnp.dot(domain_backward.T, activation_rows, preferred_element_type=jnp.float32)
        up_gradient = adapter_scale * jnp.dot(reduced_activation.T, gradient_rows, preferred_element_type=jnp.float32)
        grad_sdown = shared_scale * jnp.dot(back_shared.T, activation_rows, preferred_element_type=jnp.float32)
        grad_sup = shared_scale * jnp.dot(low_shared.T, gradient_rows, preferred_element_type=jnp.float32)
        return input_gradient.astype(jnp.bfloat16), down_gradient, up_gradient, grad_sdown, grad_sup

    input_gradient, down_gradient, up_gradient, grad_sdown, grad_sup = lax.map(per_rank, (masked, act_seq, series_domain))
    domain_picker = (series_domain[:, None] == lax.iota(jnp.int32, DOMAIN_COUNT)[None, :]).astype(jnp.float32)
    domain_down_gradient = jnp.tensordot(domain_picker, down_gradient, axes=(0, 0), precision=lax.Precision.HIGHEST)
    domain_up_gradient = jnp.tensordot(domain_picker, up_gradient, axes=(0, 0), precision=lax.Precision.HIGHEST)
    common_down_gradient = jnp.sum(grad_sdown, axis=0)
    common_up_gradient = jnp.sum(grad_sup, axis=0)
    return (input_gradient.reshape(N_DP * SERIES_TOKENS, QUERY_HEAD_WIDTH), domain_down_gradient, domain_up_gradient, common_down_gradient, common_up_gradient)
```

```python
import functools

import jax
import jax.numpy as jnp
import numpy as np
from jax import lax
from jax.experimental import pallas as pl
from jax.experimental.pallas import tpu as pltpu
from jax.sharding import Mesh
from jax.sharding import PartitionSpec as P


adapter_scale = 2.0
shared_scale = 2.0
AXES = ("y", "zl", "zh", "x", "c")
SIZES = (4, 8, 2, 4, 2)
f32 = jnp.float32
bf16 = jnp.bfloat16
NT = (((1,), (1,)), ((), ()))
NN = (((1,), (0,)), ((), ()))
TN = (((0,), (0,)), ((), ()))


def dot(a, b, dims):
    return lax.dot_general(a, b, dims, preferred_element_type=f32)


def exchange(blocks, axis):
    return lax.all_to_all(blocks, axis, 0, 0, tiled=True)


def to_all(block, axis):
    n = lax.axis_size(axis)
    return exchange(jnp.broadcast_to(block[None], (n, *block.shape)), axis)


def across(x):
    return lax.ppermute(x, "zh", [(0, 1), (1, 0)])


def matmul_kernel(half, g_ref, w_ref, o_ref):
    w = jnp.concatenate([w_ref[i] for i in range(w_ref.shape[0])], axis=1)
    o_ref[...] = dot(g_ref[...], w, NT).astype(o_ref.dtype)


def half_product(g, w, half, width):
    rows, depth = g.shape
    planes, heads, block = w.shape
    planes = planes // 2
    return pl.pallas_call(
        matmul_kernel,
        out_shape=jax.ShapeDtypeStruct((rows, heads), bf16),
        grid_spec=pltpu.PrefetchScalarGridSpec(
            num_scalar_prefetch=1,
            grid=(heads // width,),
            in_specs=[
                pl.BlockSpec((rows, depth), lambda i, h: (0, 0)),
                pl.BlockSpec((planes, width, block), lambda i, h: (h[0], i, 0)),
            ],
            out_specs=pl.BlockSpec((rows, width), lambda i, h: (0, i)),
        ),
        cost_estimate=pl.CostEstimate(
            flops=2 * rows * depth * heads,
            bytes_accessed=2 * (rows * depth + heads * depth + rows * heads),
            transcendentals=0,
        ),
        name="half_product",
    )(half.reshape(1), g, w)


def on_device(
    output_gradient,
    attention_output,
    frozen_projection,
    domain_down_map,
    domain_up_map,
    common_down_map,
    common_up_map,
    live_token_count,
    series_domain,
):
    rows, width = output_gradient.shape
    heads = attention_output.shape[1]
    ny, nzl, nx, nc = (lax.axis_size(a) for a in ("y", "zl", "x", "c"))
    nxc = nx * nc
    y, zl, zh, x, c = (lax.axis_index(a) for a in AXES)
    domains, rank, _ = domain_down_map.shape
    shared = common_down_map.shape[0]
    low = rank + shared
    half_rows = nxc * rows

    planes = lax.all_gather(frozen_projection, ("zh", "zl"), axis=0)

    positions = ((zh * nx + x) * nc + c) * rows + lax.iota(jnp.int32, rows)
    live = (positions < live_token_count[0])[:, None]
    masked = jnp.where(live, output_gradient, jnp.zeros_like(output_gradient))

    quarter = width // ny
    g = exchange(masked.reshape(rows, ny, quarter).transpose(1, 0, 2), "y")
    g = to_all(g.reshape(ny * rows, quarter), "x")
    g = jnp.stack([lax.all_gather(g[i], "c", axis=0) for i in range(nx)])
    g = g.reshape(nx, nc, ny, rows, quarter).transpose(2, 0, 1, 3, 4)
    g = g.reshape(ny * half_rows, quarter)

    domain = lax.dynamic_index_in_dim(series_domain, y * nzl + zl, 0, keepdims=False)
    up = jnp.concatenate(
        [lax.dynamic_index_in_dim(domain_up_map, domain, 0, keepdims=False), common_up_map]
    )
    down = jnp.concatenate(
        [lax.dynamic_index_in_dim(domain_down_map, domain, 0, keepdims=False), common_down_map]
    )
    far = across(jnp.concatenate([up, down]))
    far_up, far_down = far[:low], far[low:]
    first = zh == 0

    cols = masked.reshape(rows, 2, nxc, heads).transpose(2, 0, 1, 3)
    cols = exchange(cols.reshape(nxc, rows, 2 * heads), ("x", "c")).reshape(half_rows, 2 * heads)
    both_up = jnp.concatenate(
        [jnp.where(first, up, far_up), jnp.where(first, far_up, up)], axis=1
    )
    back_part = dot(both_up, cols, NT)
    low_part = dot(down, attention_output, NT)
    sums = to_all(jnp.concatenate([back_part, low_part], axis=1), ("x", "c")).sum(0)
    back_own = sums[:, :half_rows].astype(bf16)
    low_first, low_second = sums[:, half_rows : 2 * half_rows], sums[:, 2 * half_rows :]
    low_mine = jnp.where(first, low_first, low_second)
    low_far = jnp.where(first, low_second, low_first)
    got = across(jnp.concatenate([low_far, back_own.astype(f32)]))
    low_own = (low_mine + got[:low]).astype(bf16)
    back_far = got[low:].astype(bf16)
    back_all = jnp.concatenate(
        [jnp.where(first, back_own, back_far), jnp.where(first, back_far, back_own)], axis=1
    )
    down_grad = adapter_scale * dot(back_all, attention_output, NN)
    up_grad = adapter_scale * dot(low_own, cols, NN)
    up_mine = jnp.where(first, up_grad[:, :heads], up_grad[:, heads:])
    up_far = jnp.where(first, up_grad[:, heads:], up_grad[:, :heads])
    up_grad = up_mine + across(up_far)

    piece = heads // ny
    grads = jnp.concatenate([down_grad, up_grad]).reshape(2 * low, ny, piece).transpose(1, 0, 2)
    grads = exchange(grads, "y").reshape(ny, 2, low, piece)
    labels = jnp.stack(
        [
            lax.dynamic_index_in_dim(series_domain, i * nzl + zl, 0, keepdims=False)
            for i in range(ny)
        ]
    )
    picker = (labels[:, None] == lax.iota(jnp.int32, domains)[None, :]).astype(f32)
    own = (picker[:, None, :, None, None] * grads[:, :, None, :rank, :]).sum(0)
    common = grads[:, :, rank:, :].sum(0)
    packed = jnp.concatenate(
        [own.reshape(2 * domains * rank, piece), common.reshape(2 * shared, piece)]
    )
    lines = packed.shape[0]
    packed = exchange(packed.reshape(nzl, lines // nzl, piece), "zl").sum(0)
    packed = to_all(packed, "zl").reshape(lines, piece)
    packed = to_all(packed, "y").transpose(1, 0, 2).reshape(lines, heads)
    dom = domains * rank
    domain_down_gradient = packed[:dom].reshape(domains, rank, heads)
    domain_up_gradient = packed[dom : 2 * dom].reshape(domains, rank, heads)
    common_down_gradient = packed[2 * dom : 2 * dom + shared]
    common_up_gradient = packed[2 * dom + shared :]

    def finished(half, maps):
        part = half_product(g, planes, half, 256)
        part = exchange(part.reshape(ny, half_rows, heads), "y").astype(f32).sum(0)
        return (part + adapter_scale * dot(back_own, maps, TN)).astype(bf16)

    far_out = across(finished(1 - zh, far_down))
    own_out = finished(zh, down)
    grad_input = jnp.concatenate(
        [jnp.where(first, own_out, far_out), jnp.where(first, far_out, own_out)]
    )
    return (
        grad_input,
        domain_down_gradient,
        domain_up_gradient,
        common_down_gradient,
        common_up_gradient,
    )


def solution(mesh):
    inner = Mesh(np.asarray(mesh.devices).reshape(SIZES), AXES)
    dp, tensor = ("y", "zl"), ("zh", "x", "c")
    return jax.shard_map(
        on_device,
        mesh=inner,
        in_specs=(
            P(dp + tensor, None),
            P(dp, tensor),
            P(tensor, dp),
            P(None, None, tensor),
            P(None, None, tensor),
            P(None, tensor),
            P(None, tensor),
            P(dp),
            P(),
        ),
        out_specs=(
            P(dp, tensor),
            P(None, None, tensor),
            P(None, None, tensor),
            P(None, tensor),
            P(None, tensor),
        ),
        check_vma=False,
    )
```

```python
import jax
import jax.numpy as jnp
import numpy as np
from jax import lax
from jax.experimental import pallas as pl
from jax.experimental.pallas import tpu as pltpu
from jax.sharding import Mesh
from jax.sharding import PartitionSpec as P


adapter_scale = 2.0
AXES = ("y", "zl", "zh", "x", "c")
SIZES = (4, 8, 2, 4, 2)
f32 = jnp.float32
bf16 = jnp.bfloat16
NT = (((1,), (1,)), ((), ()))
NN = (((1,), (0,)), ((), ()))
TN = (((0,), (0,)), ((), ()))


def dot(a, b, dims):
    return lax.dot_general(a, b, dims, preferred_element_type=f32)


def exchange(blocks, axis):
    return lax.all_to_all(blocks, axis, 0, 0, tiled=True)


def to_all(block, axis):
    n = lax.axis_size(axis)
    return exchange(jnp.broadcast_to(block[None], (n, *block.shape)), axis)


def shifted(x, axis, step):
    n = lax.axis_size(axis)
    return lax.ppermute(x, axis, [(i, (i + step) % n) for i in range(n)])


def around(x, axis):
    return [x] + [shifted(x, axis, k) for k in range(1, lax.axis_size(axis))]


def picked(blocks, index):
    return lax.dynamic_index_in_dim(blocks, index, 0, keepdims=False)


def ordered_by(test, a, b):
    return [jnp.where(test, a, b), jnp.where(test, b, a)]


def across(x):
    return lax.ppermute(x, "zh", [(0, 1), (1, 0)])


def matmul_kernel(halves, g_ref, w_ref, *o_refs):
    w = jnp.concatenate([w_ref[i] for i in range(w_ref.shape[0])], axis=1)
    rows = o_refs[0].shape[0]
    for i, o_ref in enumerate(o_refs):
        o_ref[...] = dot(g_ref[pl.ds(i * rows, rows), :], w, NT).astype(o_ref.dtype)


def quarter_product(g, w, halves, width, parts):
    rows, depth = g.shape
    planes, heads, block = w.shape
    planes, steps = planes // 2, heads // width
    out = jax.ShapeDtypeStruct((rows // parts, 2 * heads), bf16)
    out_spec = pl.BlockSpec((rows // parts, width), lambda i, h: (0, i))
    return pl.pallas_call(
        matmul_kernel,
        out_shape=[out] * parts,
        grid_spec=pltpu.PrefetchScalarGridSpec(
            num_scalar_prefetch=1,
            grid=(2 * steps,),
            in_specs=[
                pl.BlockSpec((rows, depth), lambda i, h: (0, 0)),
                pl.BlockSpec(
                    (planes, width, block),
                    lambda i, h: (h[lax.div(i, steps)], lax.rem(i, steps), 0),
                ),
            ],
            out_specs=[out_spec] * parts,
        ),
        cost_estimate=pl.CostEstimate(
            flops=4 * rows * depth * heads,
            bytes_accessed=2 * (rows * depth + 2 * heads * depth + 2 * rows * heads),
            transcendentals=0,
        ),
        name="quarter_product",
    )(halves, g, w)


def on_device(
    output_gradient,
    attention_output,
    frozen_projection,
    domain_down_map,
    domain_up_map,
    common_down_map,
    common_up_map,
    live_token_count,
    series_domain,
):
    rows, width = output_gradient.shape
    heads = attention_output.shape[1]
    ny, nzl, nx, nc = (lax.axis_size(a) for a in ("y", "zl", "x", "c"))
    nxc = nx * nc
    y, zl, zh, x, c = (lax.axis_index(a) for a in AXES)
    domains, rank, _ = domain_down_map.shape
    shared = common_down_map.shape[0]
    low = rank + shared
    half_rows = nxc * rows

    planes = lax.all_gather(frozen_projection, ("zh", "zl"), axis=0)

    positions = ((zh * nx + x) * nc + c) * rows + lax.iota(jnp.int32, rows)
    live = (positions < live_token_count[0])[:, None]
    masked = jnp.where(live, output_gradient, jnp.zeros_like(output_gradient))

    quarter = width // ny
    domain = lax.dynamic_index_in_dim(series_domain, y * nzl + zl, 0, keepdims=False)
    up = jnp.concatenate([picked(domain_up_map, domain), common_up_map])
    down = jnp.concatenate([picked(domain_down_map, domain), common_down_map])
    first = zh == 0

    def here(x):
        return jnp.where(first, x[:, : x.shape[1] // 2], x[:, x.shape[1] // 2 :])

    def there(x):
        return jnp.where(first, x[:, x.shape[1] // 2 :], x[:, : x.shape[1] // 2])

    labels = lax.dynamic_slice_in_dim(series_domain.reshape(ny, nzl), zl, 1, axis=1)
    picker = (labels == lax.iota(jnp.int32, domains)[None, :]).astype(f32)
    low_part = dot(down, attention_output, NT)
    low_away = there(low_part)
    low_high = lax.reduce_precision(low_away, 8, 7)
    low_rest = (low_away - low_high).astype(bf16)
    far = across(jnp.concatenate([up, low_high.astype(bf16), low_rest], axis=1))
    cols = masked.reshape(rows, 2, nxc, heads).transpose(2, 0, 1, 3)
    cols = exchange(cols.reshape(nxc, rows, 2 * heads), ("x", "c"))
    g = []
    for k in range(ny):
        at = lax.rem(y + k, ny) * quarter
        block = lax.dynamic_slice_in_dim(masked, at, quarter, axis=1)
        g.append(shifted(block, "y", k) if k else block)
    g = jnp.stack(g)
    cols = cols.reshape(half_rows, 2 * heads)
    far_up, far_low = far[:, :heads], far[:, heads:].astype(f32)
    low_part = here(low_part) + far_low[:, :half_rows] + far_low[:, half_rows:]
    back_part = dot(jnp.concatenate(ordered_by(first, up, far_up), axis=1), cols, NT)
    sums = to_all(jnp.concatenate([back_part, low_part], axis=1), ("x", "c"))
    g = jnp.stack(around(g.reshape(ny * rows, quarter), "x"))
    sums = sums.sum(0).astype(bf16)
    back_own, low_own = sums[:, :half_rows], sums[:, half_rows:]
    far = across(jnp.concatenate([back_own, down], axis=1))
    up_grad = adapter_scale * dot(low_own, cols, NN)
    other = shifted(g, "c", 1)
    far, other, up_grad = lax.optimization_barrier((far, other, up_grad))
    back_far, far_down = far[:, :half_rows], far[:, half_rows:]
    back_all = jnp.concatenate(ordered_by(first, back_own, back_far), axis=1)
    down_grad = adapter_scale * dot(back_all, attention_output, NN)
    piece = heads // ny
    grads = jnp.stack(
        [
            jnp.concatenate(
                [
                    m[:, at + i * piece : at + (i + 1) * piece]
                    for m, at in ((down_grad, 0), (up_grad, 0), (up_grad, heads))
                ]
            )
            for i in range(ny)
        ]
    )
    grads = exchange(grads, "y")

    pair = jnp.stack(ordered_by(c == 0, g, other), axis=1)
    g = jnp.stack([picked(pair, lax.rem(x - i + nx, nx)) for i in range(nx)])
    g = g.reshape(nx, nc, ny, rows, quarter).transpose(2, 0, 1, 3, 4)
    g = g.reshape(ny * half_rows, quarter)

    g, grads = lax.optimization_barrier((g, grads))
    grads = grads.reshape(ny, 3, low, piece)
    own = (picker[:, None, :, None, None] * grads[:, :, None, :rank, :]).sum(0)
    common = grads[:, :, rank:, :].sum(0)
    dom, lines = domains * rank, 2 * (domains * rank + shared)
    spare = -lines % (8 * nzl)
    full = jnp.concatenate([own.reshape(3, dom, piece), common], axis=1)
    full = full.reshape(3, lines // 2, piece)
    blocks = []
    for h in range(2):
        blocks += [jnp.where(zh == h, full[0], jnp.zeros_like(full[0])), full[1 + h]]
    packed = jnp.pad(jnp.stack(blocks).reshape(2, lines, piece), ((0, 0), (0, spare), (0, 0)))
    lines = lines + spare
    packed = packed.reshape(2 * nzl, lines // nzl, piece)
    packed = exchange(packed, ("zh", "zl")).sum(0)
    packed = to_all(packed, "zl").reshape(lines, piece)
    packed = to_all(packed, "y")
    packed = jnp.concatenate([packed[i] for i in range(ny)], axis=1)
    grads = packed[: 2 * (dom + shared)].reshape(2, dom + shared, heads)
    domain_down_gradient, domain_up_gradient = grads[:, :dom].reshape(2, domains, rank, heads)
    common_down_gradient, common_up_gradient = grads[:, dom:]

    parts = quarter_product(g, planes, jnp.stack([1 - zh, zh]), 256, ny)
    parts = [shifted(parts[k], "y", -k) if k else parts[k] for k in range(ny)]

    def finished(at, maps):
        part = sum(p[:, at : at + heads].astype(f32) for p in parts)
        return (part + adapter_scale * dot(back_own, maps, TN)).astype(bf16)

    far_out = across(finished(0, far_down))
    own_out = finished(heads, down)
    grad_input = jnp.concatenate(ordered_by(first, own_out, far_out))
    return (
        grad_input,
        domain_down_gradient,
        domain_up_gradient,
        common_down_gradient,
        common_up_gradient,
    )


def solution(mesh):
    inner = Mesh(np.asarray(mesh.devices).reshape(SIZES), AXES)
    dp, tensor = ("y", "zl"), ("zh", "x", "c")

    return jax.shard_map(
        on_device,
        mesh=inner,
        in_specs=(
            P(dp + tensor, None),
            P(dp, tensor),
            P(tensor, dp),
            P(None, None, tensor),
            P(None, None, tensor),
            P(None, tensor),
            P(None, tensor),
            P(dp),
            P(),
        ),
        out_specs=(
            P(dp, tensor),
            P(None, None, tensor),
            P(None, None, tensor),
            P(None, tensor),
            P(None, tensor),
        ),
        check_vma=False,
    )
```

```python
import jax
import jax.numpy as jnp
import numpy as np
from jax import lax
from jax.experimental import pallas as pl
from jax.experimental.pallas import tpu as pltpu
from jax.sharding import Mesh
from jax.sharding import PartitionSpec as P


adapter_scale = 2.0
AXES = ("y", "zl", "zh", "x", "c")
SIZES = (4, 8, 2, 4, 2)
f32 = jnp.float32
bf16 = jnp.bfloat16
NT = (((1,), (1,)), ((), ()))
NN = (((1,), (0,)), ((), ()))
TN = (((0,), (0,)), ((), ()))


def dot(a, b, dims):
    return lax.dot_general(a, b, dims, preferred_element_type=f32)


def exchange(blocks, axis):
    return lax.all_to_all(blocks, axis, 0, 0, tiled=True)


def to_all(block, axis):
    n = lax.axis_size(axis)
    return exchange(jnp.broadcast_to(block[None], (n, *block.shape)), axis)


def shifted(x, axis, step):
    n = lax.axis_size(axis)
    return lax.ppermute(x, axis, [(i, (i + step) % n) for i in range(n)])


def around(x, axis):
    return [x] + [shifted(x, axis, k) for k in range(1, lax.axis_size(axis))]


def picked(blocks, index):
    return lax.dynamic_index_in_dim(blocks, index, 0, keepdims=False)


def ordered_by(test, a, b):
    return [jnp.where(test, a, b), jnp.where(test, b, a)]


def across(x):
    return lax.ppermute(x, "zh", [(0, 1), (1, 0)])


def matmul_kernel(half, g_ref, w_ref, *o_refs):
    w = jnp.concatenate([w_ref[i] for i in range(w_ref.shape[0])], axis=1)
    rows = o_refs[0].shape[0]
    for i, o_ref in enumerate(o_refs):
        o_ref[...] = dot(g_ref[pl.ds(i * rows, rows), :], w, NT).astype(o_ref.dtype)


def half_product(g, w, half, width, parts):
    rows, depth = g.shape
    planes, heads, block = w.shape
    planes = planes // 2
    out = jax.ShapeDtypeStruct((rows // parts, heads), bf16)
    out_spec = pl.BlockSpec((rows // parts, width), lambda i, h: (0, i))
    return pl.pallas_call(
        matmul_kernel,
        out_shape=[out] * parts,
        grid_spec=pltpu.PrefetchScalarGridSpec(
            num_scalar_prefetch=1,
            grid=(heads // width,),
            in_specs=[
                pl.BlockSpec((rows, depth), lambda i, h: (0, 0)),
                pl.BlockSpec((planes, width, block), lambda i, h: (h[0], i, 0)),
            ],
            out_specs=[out_spec] * parts,
        ),
        cost_estimate=pl.CostEstimate(
            flops=2 * rows * depth * heads,
            bytes_accessed=2 * (rows * depth + heads * depth + rows * heads),
            transcendentals=0,
        ),
        name="half_product",
    )(half.reshape(1), g, w)


def on_device(
    output_gradient,
    attention_output,
    frozen_projection,
    domain_down_map,
    domain_up_map,
    common_down_map,
    common_up_map,
    live_token_count,
    series_domain,
):
    rows, width = output_gradient.shape
    heads = attention_output.shape[1]
    ny, nzl, nx, nc = (lax.axis_size(a) for a in ("y", "zl", "x", "c"))
    nxc = nx * nc
    y, zl, zh, x, c = (lax.axis_index(a) for a in AXES)
    domains, rank, _ = domain_down_map.shape
    shared = common_down_map.shape[0]
    low = rank + shared
    half_rows = nxc * rows

    planes = lax.all_gather(frozen_projection, ("zh", "zl"), axis=0)

    positions = ((zh * nx + x) * nc + c) * rows + lax.iota(jnp.int32, rows)
    live = (positions < live_token_count[0])[:, None]
    masked = jnp.where(live, output_gradient, jnp.zeros_like(output_gradient))

    quarter = width // ny
    kinds = lax.iota(jnp.int32, domains)
    mine = lax.iota(jnp.int32, series_domain.shape[0]) == y * nzl + zl
    mine = ((series_domain[None, :] == kinds[:, None]) & mine[None, :]).any(1)

    def own_map(maps):
        return jnp.where(mine[:, None, None], maps, jnp.zeros_like(maps)).sum(0)

    up = jnp.concatenate([own_map(domain_up_map), common_up_map])
    down = jnp.concatenate([own_map(domain_down_map), common_down_map])
    first = zh == 0

    def here(x):
        return jnp.where(first, x[:, : x.shape[1] // 2], x[:, x.shape[1] // 2 :])

    def there(x):
        return jnp.where(first, x[:, x.shape[1] // 2 :], x[:, : x.shape[1] // 2])

    labels = lax.dynamic_slice_in_dim(series_domain.reshape(ny, nzl), zl, 1, axis=1)
    picker = (labels == lax.iota(jnp.int32, domains)[None, :]).astype(f32)
    low_part = dot(down, attention_output, NT)
    low_away = there(low_part)
    low_high = lax.reduce_precision(low_away, 8, 7)
    low_rest = (low_away - low_high).astype(bf16)
    far = across(jnp.concatenate([up, low_high.astype(bf16), low_rest], axis=1))
    cols = masked.reshape(rows, 2, nxc, heads).transpose(2, 0, 1, 3)
    cols = exchange(cols.reshape(nxc, rows, 2 * heads), ("x", "c"))
    g = []
    for k in range(ny):
        at = lax.rem(y + k, ny) * quarter
        block = lax.dynamic_slice_in_dim(masked, at, quarter, axis=1)
        g.append(shifted(block, "y", k) if k else block)
    g = jnp.stack(g)
    cols = cols.reshape(half_rows, 2 * heads)
    far_up, far_low = far[:, :heads], far[:, heads:].astype(f32)
    low_part = here(low_part) + far_low[:, :half_rows] + far_low[:, half_rows:]
    back_part = dot(jnp.concatenate(ordered_by(first, up, far_up), axis=1), cols, NT)
    sums = to_all(jnp.concatenate([back_part, low_part], axis=1), ("x", "c"))
    g = jnp.stack(around(g.reshape(ny * rows, quarter), "x"))
    sums = sums.sum(0).astype(bf16)
    back_own, low_own = sums[:, :half_rows], sums[:, half_rows:]
    far = across(jnp.concatenate([back_own, down], axis=1))
    up_grad = adapter_scale * dot(low_own, cols, NN)
    other = shifted(g, "c", 1)
    far, up_grad = lax.optimization_barrier((far, up_grad))
    back_far, far_down = far[:, :half_rows], far[:, half_rows:]
    back_all = jnp.concatenate(ordered_by(first, back_own, back_far), axis=1)
    down_grad = adapter_scale * dot(back_all, attention_output, NN)
    piece = heads // ny
    grads = jnp.stack(
        [
            jnp.concatenate(
                [
                    m[:, at + i * piece : at + (i + 1) * piece]
                    for m, at in ((down_grad, 0), (up_grad, 0), (up_grad, heads))
                ]
            )
            for i in range(ny)
        ]
    )
    grads = exchange(grads, "y")

    pair = jnp.stack(ordered_by(c == 0, g, other), axis=1)
    g = jnp.stack([picked(pair, lax.rem(x - i + nx, nx)) for i in range(nx)])
    g = g.reshape(nx, nc, ny, rows, quarter).transpose(2, 0, 1, 3, 4)
    g = g.reshape(ny * half_rows, quarter)

    g, grads = lax.optimization_barrier((g, grads))
    grads = grads.reshape(ny, 3, low, piece)
    own = (picker[:, None, :, None, None] * grads[:, :, None, :rank, :]).sum(0)
    common = grads[:, :, rank:, :].sum(0)
    dom, lines = domains * rank, 2 * (domains * rank + shared)
    spare = -lines % (8 * nzl)
    full = jnp.concatenate([own.reshape(3, dom, piece), common], axis=1)
    full = full.reshape(3, lines // 2, piece)
    blocks = []
    for h in range(2):
        blocks += [jnp.where(zh == h, full[0], jnp.zeros_like(full[0])), full[1 + h]]
    packed = jnp.pad(jnp.stack(blocks).reshape(2, lines, piece), ((0, 0), (0, spare), (0, 0)))
    lines = lines + spare
    packed = packed.reshape(2 * nzl, lines // nzl, piece)
    packed = exchange(packed.astype(bf16), ("zh", "zl")).astype(f32).sum(0)
    packed = to_all(packed.astype(bf16), "zl").reshape(lines, piece)
    packed = to_all(packed, "y")
    packed = jnp.concatenate([packed[i] for i in range(ny)], axis=1).astype(f32)
    grads = packed[: 2 * (dom + shared)].reshape(2, dom + shared, heads)
    domain_down_gradient, domain_up_gradient = grads[:, :dom].reshape(2, domains, rank, heads)
    common_down_gradient, common_up_gradient = grads[:, dom:]

    def finished(half, maps):
        parts = list(half_product(g, planes, half, 256, ny))
        for k in range(1, ny):
            parts[k] = shifted(parts[k], "y", -k)
        part = sum(p.astype(f32) for p in parts)
        return (part + adapter_scale * dot(back_own, maps, TN)).astype(bf16)

    far_out = finished(1 - zh, far_down)
    far_out = across(far_out)
    own_out = finished(zh, down)
    grad_input = jnp.concatenate(ordered_by(first, own_out, far_out))
    return (
        grad_input,
        domain_down_gradient,
        domain_up_gradient,
        common_down_gradient,
        common_up_gradient,
    )


def solution(mesh):
    inner = Mesh(np.asarray(mesh.devices).reshape(SIZES), AXES)
    dp, tensor = ("y", "zl"), ("zh", "x", "c")

    return jax.shard_map(
        on_device,
        mesh=inner,
        in_specs=(
            P(dp + tensor, None),
            P(dp, tensor),
            P(tensor, dp),
            P(None, None, tensor),
            P(None, None, tensor),
            P(None, tensor),
            P(None, tensor),
            P(dp),
            P(),
        ),
        out_specs=(
            P(dp, tensor),
            P(None, None, tensor),
            P(None, None, tensor),
            P(None, tensor),
            P(None, tensor),
        ),
        check_vma=False,
    )
```

```python
import jax
import jax.numpy as jnp
import numpy as np
from jax import lax
from jax.experimental import pallas as pl
from jax.experimental.pallas import tpu as pltpu
from jax.sharding import Mesh
from jax.sharding import PartitionSpec as P


adapter_scale = 2.0
AXES = ("y", "zl", "zh", "x", "c")
SIZES = (4, 8, 2, 4, 2)
f32 = jnp.float32
bf16 = jnp.bfloat16
NT = (((1,), (1,)), ((), ()))
NN = (((1,), (0,)), ((), ()))
TN = (((0,), (0,)), ((), ()))


def dot(a, b, dims):
    return lax.dot_general(a, b, dims, preferred_element_type=f32)


def exchange(blocks, axis):
    return lax.all_to_all(blocks, axis, 0, 0, tiled=True)


def to_all(block, axis):
    n = lax.axis_size(axis)
    return exchange(jnp.broadcast_to(block[None], (n, *block.shape)), axis)


def shifted(x, axis, step):
    n = lax.axis_size(axis)
    return lax.ppermute(x, axis, [(i, (i + step) % n) for i in range(n)])


def around(x, axis):
    return [x] + [shifted(x, axis, k) for k in range(1, lax.axis_size(axis))]


def picked(blocks, index):
    return lax.dynamic_index_in_dim(blocks, index, 0, keepdims=False)


def ordered_by(test, a, b):
    return [jnp.where(test, a, b), jnp.where(test, b, a)]


def across(x):
    return lax.ppermute(x, "zh", [(0, 1), (1, 0)])


def matmul_kernel(half, g_ref, w_ref, *o_refs):
    w = jnp.concatenate([w_ref[i] for i in range(w_ref.shape[0])], axis=1)
    rows = o_refs[0].shape[0]
    for i, o_ref in enumerate(o_refs):
        o_ref[...] = dot(g_ref[pl.ds(i * rows, rows), :], w, NT).astype(o_ref.dtype)


def half_product(g, w, half, width, parts):
    rows, depth = g.shape
    planes, heads, block = w.shape
    planes = planes // 2
    out = jax.ShapeDtypeStruct((rows // parts, heads), bf16)
    out_spec = pl.BlockSpec((rows // parts, width), lambda i, h: (0, i))
    return pl.pallas_call(
        matmul_kernel,
        out_shape=[out] * parts,
        grid_spec=pltpu.PrefetchScalarGridSpec(
            num_scalar_prefetch=1,
            grid=(heads // width,),
            in_specs=[
                pl.BlockSpec((rows, depth), lambda i, h: (0, 0)),
                pl.BlockSpec((planes, width, block), lambda i, h: (h[0], i, 0)),
            ],
            out_specs=[out_spec] * parts,
        ),
        cost_estimate=pl.CostEstimate(
            flops=2 * rows * depth * heads,
            bytes_accessed=2 * (rows * depth + heads * depth + rows * heads),
            transcendentals=0,
        ),
        name="half_product",
    )(half.reshape(1), g, w)


def on_device(
    output_gradient,
    attention_output,
    frozen_projection,
    domain_down_map,
    domain_up_map,
    common_down_map,
    common_up_map,
    live_token_count,
    series_domain,
):
    rows, width = output_gradient.shape
    heads = attention_output.shape[1]
    ny, nzl, nx, nc = (lax.axis_size(a) for a in ("y", "zl", "x", "c"))
    nxc = nx * nc
    y, zl, zh, x, c = (lax.axis_index(a) for a in AXES)
    domains, rank, _ = domain_down_map.shape
    shared = common_down_map.shape[0]
    low = rank + shared
    half_rows = nxc * rows

    planes = lax.all_gather(frozen_projection, ("zh", "zl"), axis=0)

    positions = ((zh * nx + x) * nc + c) * rows + lax.iota(jnp.int32, rows)
    live = (positions < live_token_count[0])[:, None]
    masked = jnp.where(live, output_gradient, jnp.zeros_like(output_gradient))

    quarter = width // ny
    kinds = lax.iota(jnp.int32, domains)
    at_own = lax.iota(jnp.int32, series_domain.shape[0]) == y * nzl + zl
    own_kind = ((series_domain[None, :] == kinds[:, None]) & at_own[None, :]).any(1)

    def own_map(maps):
        return jnp.where(own_kind[:, None, None], maps, jnp.zeros_like(maps)).sum(0)

    up = jnp.concatenate([own_map(domain_up_map), common_up_map])
    down = jnp.concatenate([own_map(domain_down_map), common_down_map])
    first = zh == 0

    def here(x):
        return jnp.where(first, x[:, : x.shape[1] // 2], x[:, x.shape[1] // 2 :])

    def there(x):
        return jnp.where(first, x[:, x.shape[1] // 2 :], x[:, : x.shape[1] // 2])

    labels = lax.dynamic_slice_in_dim(series_domain.reshape(ny, nzl), zl, 1, axis=1)
    picker = (labels == lax.iota(jnp.int32, domains)[None, :]).astype(f32)
    low_part = dot(down, attention_output, NT)
    low_away = there(low_part)
    low_high = lax.reduce_precision(low_away, 8, 7)
    low_rest = (low_away - low_high).astype(bf16)
    far = across(jnp.concatenate([up, low_high.astype(bf16), low_rest], axis=1))
    cols = masked.reshape(rows, 2, nxc, heads).transpose(2, 0, 1, 3)
    cols = exchange(cols.reshape(nxc, rows, 2 * heads), ("x", "c"))
    g = []
    for k in range(ny):
        at = lax.rem(y + k, ny) * quarter
        block = lax.dynamic_slice_in_dim(masked, at, quarter, axis=1)
        g.append(shifted(block, "y", k) if k else block)
    g = jnp.stack(g)
    cols = cols.reshape(half_rows, 2 * heads)
    far_up, far_low = far[:, :heads], far[:, heads:].astype(f32)
    low_part = here(low_part) + far_low[:, :half_rows] + far_low[:, half_rows:]
    back_part = dot(jnp.concatenate(ordered_by(first, up, far_up), axis=1), cols, NT)
    sums = to_all(jnp.concatenate([back_part, low_part], axis=1), ("x", "c"))
    g = jnp.stack(around(g.reshape(ny * rows, quarter), "x"))
    sums = sums.sum(0).astype(bf16)
    back_own, low_own = sums[:, :half_rows], sums[:, half_rows:]
    far = across(jnp.concatenate([back_own, down], axis=1))
    up_grad = adapter_scale * dot(low_own, cols, NN)
    other = shifted(g, "c", 1)
    far, up_grad = lax.optimization_barrier((far, up_grad))
    back_far, far_down = far[:, :half_rows], far[:, half_rows:]
    back_all = jnp.concatenate(ordered_by(first, back_own, back_far), axis=1)
    down_grad = adapter_scale * dot(back_all, attention_output, NN)
    piece = heads // ny
    grads = jnp.stack(
        [
            jnp.concatenate(
                [
                    m[:, at + i * piece : at + (i + 1) * piece]
                    for m, at in ((down_grad, 0), (up_grad, 0), (up_grad, heads))
                ]
            )
            for i in range(ny)
        ]
    )
    grads = exchange(grads, "y")

    pair = jnp.stack(ordered_by(c == 0, g, other), axis=1)
    g = jnp.stack([picked(pair, lax.rem(x - i + nx, nx)) for i in range(nx)])
    g = g.reshape(nx, nc, ny, rows, quarter).transpose(2, 0, 1, 3, 4)
    g = g.reshape(ny * half_rows, quarter)

    g, grads = lax.optimization_barrier((g, grads))
    grads = grads.reshape(ny, 3, low, piece)
    own = (picker[:, None, :, None, None] * grads[:, :, None, :rank, :]).sum(0)
    common = grads[:, :, rank:, :].sum(0)
    dom, lines = domains * rank, 2 * (domains * rank + shared)
    spare = -lines % (8 * nzl)
    full = jnp.concatenate([own.reshape(3, dom, piece), common], axis=1)
    full = full.reshape(3, lines // 2, piece)
    blocks = []
    for h in range(2):
        blocks += [jnp.where(zh == h, full[0], jnp.zeros_like(full[0])), full[1 + h]]
    packed = jnp.pad(jnp.stack(blocks).reshape(2, lines, piece), ((0, 0), (0, spare), (0, 0)))
    lines = lines + spare
    packed = packed.reshape(2 * nzl, lines // nzl, piece)
    packed = exchange(packed.astype(bf16), ("zh", "zl")).astype(f32).sum(0)
    packed = to_all(packed.astype(bf16), "zl").reshape(lines, piece)
    packed = to_all(packed, "y")
    packed = jnp.concatenate([packed[i] for i in range(ny)], axis=1).astype(f32)
    grads = packed[: 2 * (dom + shared)].reshape(2, dom + shared, heads)
    domain_down_gradient, domain_up_gradient = grads[:, :dom].reshape(2, domains, rank, heads)
    common_down_gradient, common_up_gradient = grads[:, dom:]

    def finished(half, maps):
        parts = list(half_product(g, planes, half, 256, ny))
        for k in range(1, ny):
            parts[k] = shifted(parts[k], "y", -k)
        part = sum(p.astype(f32) for p in parts)
        return (part + adapter_scale * dot(back_own, maps, TN)).astype(bf16)

    far_out = finished(1 - zh, far_down)
    far_out = across(far_out)
    own_out = finished(zh, down)
    mine = (lax.iota(jnp.int32, 2) == zh)[:, None, None]
    grad_input = jnp.where(mine, own_out[None], far_out[None]).reshape(2 * half_rows, heads)
    return (
        grad_input,
        domain_down_gradient,
        domain_up_gradient,
        common_down_gradient,
        common_up_gradient,
    )


def solution(mesh):
    inner = Mesh(np.asarray(mesh.devices).reshape(SIZES), AXES)
    dp, tensor = ("y", "zl"), ("zh", "x", "c")

    return jax.shard_map(
        on_device,
        mesh=inner,
        in_specs=(
            P(dp + tensor, None),
            P(dp, tensor),
            P(tensor, dp),
            P(None, None, tensor),
            P(None, None, tensor),
            P(None, tensor),
            P(None, tensor),
            P(dp),
            P(),
        ),
        out_specs=(
            P(dp, tensor),
            P(None, None, tensor),
            P(None, None, tensor),
            P(None, tensor),
            P(None, tensor),
        ),
        check_vma=False,
    )
```
